32 devices in a mesh: dp: 8 (over y, x, core), mp: 4 (over z).
Axes of the slice: x: 2, y: 2, z: 4, core: 2. Of those that a mesh axis runs over, the one named last changes fastest.
Arguments:
- tokens: bfloat16 [16384, 2048], P(('dp', 'mp')), may hold values from -6 to 6
- segment_ids: int32 [16384], P('dp'), may hold values from 0 to 1, as said below
- grad_out: bfloat16 [16384, 2048], P(('dp', 'mp')), may hold values from -6 to 6
- attn_gain: bfloat16 [2048], replicated, may hold values from 0.5 to 1.5
- w_query: bfloat16 [2048, 2048], P(None, 'mp'), may hold values from -0.125 to 0.125
- w_key: bfloat16 [2048, 512], P(None, 'mp'), may hold values from -0.125 to 0.125
- w_value: bfloat16 [2048, 512], P(None, 'mp'), may hold values from -0.125 to 0.125
- w_output: bfloat16 [2048, 2048], P('mp'), may hold values from -0.75 to 0.75
- ffn_gain: bfloat16 [2048], replicated, may hold values from 0.5 to 1.5
- w_gate: bfloat16 [2048, 8192], P(None, 'mp'), may hold values from -0.125 to 0.125
- w_up: bfloat16 [2048, 8192], P(None, 'mp'), may hold values from -0.125 to 0.125
- w_down: bfloat16 [8192, 2048], P('mp'), may hold values from -0.0625 to 0.0625
Outputs:
- layer_out: bfloat16 [16384, 2048], P(('dp', 'mp'))
- grad_tokens: bfloat16 [16384, 2048], P(('dp', 'mp'))
- grad_attn_gain: float32 [2048], replicated
- grad_w_query: float32 [2048, 2048], P('dp', 'mp')
- grad_w_key: float32 [2048, 512], P('dp', 'mp')
- grad_w_value: float32 [2048, 512], P('dp', 'mp')
- grad_w_output: float32 [2048, 2048], P('mp', 'dp')
- grad_ffn_gain: float32 [2048], replicated
- grad_w_gate: float32 [2048, 8192], P('dp', 'mp')
- grad_w_up: float32 [2048, 8192], P('dp', 'mp')
- grad_w_down: float32 [8192, 2048], P('mp', 'dp')
The draws below stay inside these ranges and needn't reach their ends.
Inputs may be any that keep to these rules, and one draw needn't show every extreme that they name: `segment_ids`: each block of 2048 rows (one index of dp) holds whole sequences numbered from 0 in order; every length is a multiple of 1024; in one block a single sequence fills all 2048 rows, in another every sequence has 1024 rows.
All inputs are finite; a program needn't handle non-finite values.
Results may differ from the reference program's by a relative error of at most 0.02.
Values may be sent and summed in bfloat16 or wider, within the bound.
No kernel may reach another device: no remote copies, remote signals or barrier semaphores. Data moves between devices by JAX's collectives and lax.ppermute only.
A program may use at most 320 MiB of HBM per device.

```python
import math
import jax
import jax.numpy as jnp
from jax import lax

D = 2048
H = 32
KV = 8
HD = 64
FF = 8192
GRP = 2048
MIN_SEQ = 1024
TOKENS = 16384


def draw_segment_ids(key, part):
    group_count = TOKENS // GRP
    piece_count = GRP // MIN_SEQ
    start_flags = jax.random.randint(jax.random.fold_in(key, 11), (group_count, piece_count), 0, 2)
    whole_group = jax.random.randint(jax.random.fold_in(key, 12), (), 0, group_count)
    offset = jax.random.randint(jax.random.fold_in(key, 13), (), 1, group_count)
    split_group = (whole_group + offset) % group_count
    group_index = jnp.arange(group_count)[:, None]
    start_flags = jnp.where(group_index == whole_group, 0, start_flags)
    start_flags = jnp.where(group_index == split_group, 1, start_flags)
    start_flags = start_flags.at[:, 0].set(0)
    seq_numbers = jnp.cumsum(start_flags, axis=1)
    return jnp.repeat(seq_numbers, MIN_SEQ, axis=1).reshape(TOKENS).astype(jnp.int32)


def with_spikes(result, key, source, target, parts, factor):
    owner, partner = [(jnp.arange(result.shape[axis_at]) // (result.shape[axis_at] // parts)).reshape([-1 if axis == axis_at else 1 for axis in range(result.ndim)]) for axis_at in (source, target)]
    chosen = jax.random.permutation(key, parts)[partner]
    strong = (owner == chosen) | (owner == (partner + parts // 2) % parts)
    return jnp.where(strong, factor * result, result)


def shard_levels(stream_key, extent, shards, smallest, high):
    level = 1.0
    for axis_at, blocks in shards:
        draws = jax.random.uniform(jax.random.fold_in(jax.random.fold_in(stream_key, 6), axis_at), (blocks,), jnp.float32, smallest / len(shards), high / len(shards))
        level = level * jnp.repeat(jnp.exp(draws), extent[axis_at] // blocks).reshape((-1,) + (1,) * (len(extent) - 1 - axis_at))
    return level


def noise(rng, dims, width, most, shards=(), kind=jnp.bfloat16):
    values = width * jax.random.normal(rng, dims, jnp.float32)
    if shards:
        values = values * shard_levels(rng, dims, shards, -0.22, 0.18)
    return jnp.clip(values, -most, most).astype(kind)


def heavy_noise(stream_key, extent, scale, bound, cuts, heavy, held_as=jnp.bfloat16):
    result = scale * jax.random.normal(stream_key, extent, jnp.float32)
    if cuts:
        result = result * shard_levels(stream_key, extent, cuts, -0.22, 0.18)
    return jnp.clip(with_spikes(result, jax.random.fold_in(stream_key, 3), *heavy), -bound, bound).astype(held_as)


def setup_inputs(seed: int = 0) -> dict:
    arg_keys = jax.random.split(jax.random.key(seed), 13)
    tokens = noise(arg_keys[0], (TOKENS, D), 1.0, 6.0, ((0, 32),))
    segment_ids = draw_segment_ids(jax.random.fold_in(arg_keys[12], 71), 0)
    grad_out = heavy_noise(arg_keys[2], (TOKENS, D), 1.0, 6.0, ((0, 32),), (0, 1, 32, 2.75))
    attn_gain = jnp.clip(1.0 + 0.1 * jax.random.normal(arg_keys[3], (D,), jnp.float32), 0.5, 1.5).astype(jnp.bfloat16)
    w_query = noise(arg_keys[4], (D, H * HD), D ** -0.5, 0.125, ((1, 4),))
    w_key = noise(arg_keys[5], (D, KV * HD), D ** -0.5, 0.125, ((1, 4),))
    w_value = noise(arg_keys[6], (D, KV * HD), D ** -0.5, 0.125, ((1, 4),))
    w_output = noise(arg_keys[7], (H * HD, D), (H * HD // 32) ** -0.5, 0.75, ((0, 4),))
    ffn_gain = jnp.clip(1.0 + 0.1 * jax.random.normal(arg_keys[8], (D,), jnp.float32), 0.5, 1.5).astype(jnp.bfloat16)
    w_gate = noise(arg_keys[9], (D, FF), D ** -0.5, 0.125, ((1, 4),))
    w_up = noise(arg_keys[10], (D, FF), D ** -0.5, 0.125, ((1, 4),))
    w_down = noise(arg_keys[11], (FF, D), FF ** -0.5, 0.0625, ((0, 4),))
    return dict(tokens=tokens, segment_ids=segment_ids, grad_out=grad_out, attn_gain=attn_gain, w_query=w_query, w_key=w_key, w_value=w_value, w_output=w_output, ffn_gain=ffn_gain, w_gate=w_gate, w_up=w_up, w_down=w_down)


@jax.custom_vjp
def low(v):
    return lax.optimization_barrier(v.astype(jnp.bfloat16)).astype(jnp.float32)

@jax.custom_vjp
def low_back(v):
    return v

def low_keep(v):
    return (low(v), None)

def low_pass(kept, grad):
    return (grad,)

def back_keep(v):
    return (v, None)

def back_low(kept, grad):
    return (low(grad),)
low.defvjp(low_keep, low_pass)
low_back.defvjp(back_keep, back_low)
norm_eps = 1e-05
score_scale = 0.125
highest = lax.Precision.HIGHEST

def rope_table(places):
    half_dim = HD // 2
    freq_index = jnp.arange(half_dim, dtype=jnp.float32)
    base_freq = jnp.power(jnp.float32(500000.0), -2.0 * freq_index / HD)
    wave_len = 2.0 * math.pi / base_freq
    smooth = (8192.0 / wave_len - 1.0) / 3.0
    blended = (1.0 - smooth) * base_freq / 32.0 + smooth * base_freq
    frequency = jnp.where(wave_len < 2048.0, base_freq, jnp.where(wave_len > 8192.0, base_freq / 32.0, blended))
    angles = places[:, None] * frequency[None, :]
    cos_table = jnp.concatenate([jnp.cos(angles), jnp.cos(angles)], axis=-1)
    sin_table = jnp.concatenate([jnp.sin(angles), jnp.sin(angles)], axis=-1)
    return (cos_table, sin_table)

def places_of(segment):
    row_count = segment.shape[0]
    row_index = jnp.arange(row_count, dtype=jnp.int32)
    new_start = jnp.concatenate([jnp.ones((1,), dtype=jnp.bool_), segment[1:] != segment[:-1]])
    first_row = lax.cummax(jnp.where(new_start, row_index, 0), axis=0)
    return ((row_index - first_row).astype(jnp.float32), row_index)

def rotate(values, cos_table, sin_table):
    half_dim = values.shape[-1] // 2
    turned = jnp.concatenate([-values[..., half_dim:], values[..., :half_dim]], axis=-1)
    return values * cos_table[:, None, :] + turned * sin_table[:, None, :]

def rms_scale(values, gain_vec):
    return values * lax.rsqrt(lax.optimization_barrier(jnp.mean(values * values, axis=-1, keepdims=True)) + norm_eps) * gain_vec

def group_forward(row_data, segment, weights):
    w_query, w_key, w_value, w_output, w_gate, w_up, w_down, attn_gain, ffn_gain = weights
    row_count = row_data.shape[0]
    normed_one = low(rms_scale(row_data, attn_gain))
    query_raw = low_back(jnp.dot(normed_one, w_query, precision=highest))
    key_raw = low_back(jnp.dot(normed_one, w_key, precision=highest))
    value_low = low(low_back(jnp.dot(normed_one, w_value, precision=highest))).reshape(row_count, KV, HD)
    places, row_index = places_of(segment)
    cos_table, sin_table = rope_table(places)
    query_rot = low(rotate(query_raw.reshape(row_count, H, HD), cos_table, sin_table))
    key_rot = low(rotate(key_raw.reshape(row_count, KV, HD), cos_table, sin_table))
    block_rows = min(512, row_count)
    block_count = row_count // block_rows
    query_blocks = query_rot.reshape(block_count, block_rows, KV, H // KV, HD)
    seg_blocks = segment.reshape(block_count, block_rows)
    index_blocks = row_index.reshape(block_count, block_rows)

    def attend(pieces):
        query_block, seg_block, index_block = pieces
        scores = low_back(jnp.einsum('qgrd,kgd->grqk', query_block, key_rot, precision=highest) * score_scale)
        allowed = (seg_block[:, None] == segment[None, :]) & (index_block[:, None] >= row_index[None, :])
        scores = jnp.where(allowed, scores, -1e+30)
        row_max = lax.optimization_barrier(jnp.max(scores, axis=-1, keepdims=True))
        raised = jnp.exp(scores - row_max)
        chance = raised / lax.optimization_barrier(jnp.sum(raised, axis=-1, keepdims=True))
        return jnp.einsum('grqk,kgd->qgrd', low(chance), value_low, precision=highest)
    attended = lax.map(jax.checkpoint(attend), (query_blocks, seg_blocks, index_blocks))
    attn_low = low(low_back(attended.reshape(row_count, H * HD)))
    attn_branch = low_back(jnp.dot(attn_low, w_output, precision=highest))
    mid_rows = row_data + attn_branch
    normed_two = low(rms_scale(mid_rows, ffn_gain))
    gate_act = low_back(jnp.dot(normed_two, w_gate, precision=highest))
    up_act = low_back(jnp.dot(normed_two, w_up, precision=highest))
    hidden = low(jax.nn.silu(gate_act) * up_act)
    ffn_branch = low_back(jnp.dot(hidden, w_down, precision=highest))
    return mid_rows + ffn_branch

def reference(tokens, segment_ids, grad_out, attn_gain, w_query, w_key, w_value, w_output, ffn_gain, w_gate, w_up, w_down):
    group_count = tokens.shape[0] // GRP
    params = tuple((member.astype(jnp.float32) for member in (w_query, w_key, w_value, w_output, w_gate, w_up, w_down, attn_gain, ffn_gain)))
    row_data = tokens.astype(jnp.float32).reshape(group_count, GRP, D)
    seg_groups = segment_ids.reshape(group_count, GRP)

    def forward(row_input, weights):

        def one_group(pieces):
            return group_forward(pieces[0], pieces[1], weights)
        return lax.map(jax.checkpoint(one_group), (row_input, seg_groups))
    layer_out, pullback = jax.vjp(forward, row_data, params)
    grad_rows, grad_params = pullback(grad_out.astype(jnp.float32).reshape(group_count, GRP, D))
    grad_query, grad_key, grad_value, grad_output, grad_gate, grad_up, grad_down, grad_gain_one, grad_gain_two = grad_params
    return (layer_out.reshape(-1, D).astype(jnp.bfloat16), grad_rows.reshape(-1, D).astype(jnp.bfloat16), grad_gain_one, grad_query, grad_key, grad_value, grad_output, grad_gain_two, grad_gate, grad_up, grad_down)
```

```python
import functools
import math

import jax
import jax.numpy as jnp
from jax import lax
from jax.experimental import pallas as pl
from jax.experimental.pallas import tpu as pltpu
from jax.sharding import PartitionSpec as P

HD = 64
LANES = 128
UNIT = 1024
BF = jnp.bfloat16
F32 = jnp.float32

norm_eps = 1e-05
score_scale = 0.125

NT = (((1,), (1,)), ((), ()))
TN = (((0,), (0,)), ((), ()))
NN = (((1,), (0,)), ((), ()))
VMEM_LIMIT = 60 * 1024 * 1024


def mm(a, b, dims=NN):
    return lax.dot_general(a, b, dims, preferred_element_type=F32)


def call(body, *, flops, nbytes, trans=0, **kw):
    return pl.pallas_call(
        body,
        compiler_params=pltpu.CompilerParams(vmem_limit_bytes=VMEM_LIMIT),
        cost_estimate=pl.CostEstimate(flops=flops, bytes_accessed=nbytes, transcendentals=trans),
        **kw,
    )


def rope_table(places):
    half_dim = HD // 2
    freq_index = jnp.arange(half_dim, dtype=jnp.float32)
    base_freq = jnp.power(jnp.float32(500000.0), -2.0 * freq_index / HD)
    wave_len = 2.0 * math.pi / base_freq
    smooth = (8192.0 / wave_len - 1.0) / 3.0
    blended = (1.0 - smooth) * base_freq / 32.0 + smooth * base_freq
    frequency = jnp.where(
        wave_len < 2048.0, base_freq, jnp.where(wave_len > 8192.0, base_freq / 32.0, blended)
    )
    angles = places[:, None] * jnp.tile(frequency, LANES // half_dim)[None, :]
    return jnp.cos(angles), jnp.sin(angles)


def turn(t, cos_t, sin_t):
    lane = lax.broadcasted_iota(jnp.int32, t.shape, 1)
    first = (lane % HD) < (HD // 2)
    rot = jnp.where(first, -pltpu.roll(t, LANES - HD // 2, 1), pltpu.roll(t, HD // 2, 1))
    return t * cos_t + rot * sin_t


def qkv_body(n1_ref, w_ref, cos_ref, sin_ref, q_ref, kv_ref, *, qc, kc):
    parts, _, rows, cols = w_ref.shape
    y = mm(n1_ref[...], w_ref[...].reshape(parts * rows, cols))
    cos_t, sin_t = cos_ref[...], sin_ref[...]
    for c in range(0, qc, LANES):
        q_ref[:, c : c + LANES] = (
            turn(y[:, c : c + LANES], cos_t, sin_t) * score_scale
        ).astype(BF)
    if kc >= LANES:
        for c in range(0, kc, LANES):
            kv_ref[:, c : c + LANES] = turn(
                y[:, qc + c : qc + c + LANES], cos_t, sin_t
            ).astype(BF)
        kv_ref[:, kc:] = y[:, qc + kc :].astype(BF)
    else:
        both = y[:, qc : qc + LANES]
        lane = lax.broadcasted_iota(jnp.int32, both.shape, 1)
        kv_ref[...] = jnp.where(lane < kc, turn(both, cos_t, sin_t), both).astype(BF)


def qkv_call(n1, wqkv, cos_t, sin_t, qc, kc):
    rows, width = n1.shape
    dps, n, wr, cols = wqkv.shape
    return call(
        functools.partial(qkv_body, qc=qc, kc=kc),
        flops=2 * rows * width * n * cols,
        nbytes=2 * width * n * cols + 4 * rows * width,
        grid=(n,),
        in_specs=[
            pl.BlockSpec((rows, width), lambda j: (0, 0)),
            pl.BlockSpec((dps, 1, wr, cols), lambda j: (0, j, 0, 0)),
            pl.BlockSpec((rows, LANES), lambda j: (0, 0)),
            pl.BlockSpec((rows, LANES), lambda j: (0, 0)),
        ],
        out_specs=[
            pl.BlockSpec((rows, qc), lambda j: (0, j)),
            pl.BlockSpec((rows, 2 * kc), lambda j: (0, j)),
        ],
        out_shape=[
            jax.ShapeDtypeStruct((rows, n * qc), BF),
            jax.ShapeDtypeStruct((rows, n * 2 * kc), BF),
        ],
        name="qkv",
    )(n1, wqkv, cos_t, sin_t)


def half_views(x, half):
    wide = x.astype(F32)
    lane = lax.broadcasted_iota(jnp.int32, wide.shape, 1)
    kept = jnp.where((lane // HD) == half, wide, 0.0)
    moved = pltpu.roll(kept, HD, 1)
    low = jnp.where(half == 0, kept, moved)
    high = jnp.where(half == 0, moved, kept)
    return low.astype(BF), high.astype(BF)


def placed_views(x, half):
    wide = x.astype(F32)
    lane = lax.broadcasted_iota(jnp.int32, wide.shape, 1)
    swapped = pltpu.roll(wide, HD, 1)
    keep = (lane // HD) == half
    first = jnp.where(keep, jnp.where(half == 0, wide, swapped), 0.0)
    second = jnp.where(keep, jnp.where(half == 0, swapped, wide), 0.0)
    return first.astype(BF), second.astype(BF)


def fwd_body(info_ref, q_ref, *refs, n, tiles_per_kv):
    kv_refs = refs[:n]
    o_ref, lse_ref, m_sc, l_sc, acc_sc = refs[n:]
    i = pl.program_id(0)
    half = (i // tiles_per_kv) % 2
    count = info_ref[0]
    q = q_ref[...]
    rows = q.shape[0]
    upper = lax.broadcasted_iota(jnp.int32, (LANES, rows), 0) < HD

    def part(s):
        kv = kv_refs[s]
        ks = half_views(kv[:, :LANES], half)
        vs = half_views(kv[:, LANES:], half)
        added = None
        factors = []
        for h in range(2):
            scores = mm(ks[h], q, NT)
            if s == 0:
                key_at = lax.broadcasted_iota(jnp.int32, scores.shape, 0)
                row_at = lax.broadcasted_iota(jnp.int32, scores.shape, 1)
                scores = jnp.where(key_at <= row_at, scores, -1e30)
            top = jnp.max(scores, axis=0, keepdims=True)
            if s > 0:
                old = m_sc[h : h + 1, :]
                top = jnp.maximum(top, old)
            raised = jnp.exp(scores - top)
            total = jnp.sum(raised, axis=0, keepdims=True)
            if s > 0:
                factor = jnp.exp(old - top)
                factors.append(factor)
                total = total + l_sc[h : h + 1, :] * factor
            m_sc[h : h + 1, :] = top
            l_sc[h : h + 1, :] = total
            piece = mm(vs[h], raised.astype(BF), TN)
            added = piece if added is None else added + piece
        if s > 0:
            added = added + acc_sc[...] * jnp.where(upper, factors[0], factors[1])
        acc_sc[...] = added

    part(0)
    for s in range(1, n):
        pl.when(s <= count)(functools.partial(part, s))
    sums = l_sc[...]
    done = acc_sc[...] / jnp.where(upper, sums[0:1, :], sums[1:2, :])
    o_ref[...] = done.T.astype(BF)
    lse_ref[0] = m_sc[...] + jnp.log(sums)


def fwd_call(info, q, kvs):
    rows, width = q.shape
    n = len(kvs)
    tiles = width // LANES
    pairs = kvs[0].shape[1] // (2 * LANES)
    per_pair = tiles // pairs
    return call(
        functools.partial(fwd_body, n=n, tiles_per_kv=per_pair // 2),
        flops=4 * rows * rows * n * width,
        nbytes=4 * rows * width + 2 * n * rows * kvs[0].shape[1],
        trans=rows * rows * n * width // HD,
        grid_spec=pltpu.PrefetchScalarGridSpec(
            num_scalar_prefetch=1,
            grid=(tiles,),
            in_specs=[pl.BlockSpec((rows, LANES), lambda i, _: (0, i))]
            + [pl.BlockSpec((rows, 2 * LANES), lambda i, _: (0, i // per_pair))] * n,
            out_specs=[
                pl.BlockSpec((rows, LANES), lambda i, _: (0, i)),
                pl.BlockSpec((1, 8, rows), lambda i, _: (i, 0, 0)),
            ],
            scratch_shapes=[
                pltpu.VMEM((8, rows), F32),
                pltpu.VMEM((8, rows), F32),
                pltpu.VMEM((LANES, rows), F32),
            ],
        ),
        out_shape=[
            jax.ShapeDtypeStruct((rows, width), BF),
            jax.ShapeDtypeStruct((tiles, 8, rows), F32),
        ],
        name="attend",
    )(info, q, *kvs)


def bwd_body(info_ref, q_ref, do_ref, o_ref, lse_ref, *refs, dists, per_pair, first, last):
    refs = list(refs)
    kv_refs = [refs.pop(0) for _ in dists]
    before_ref = None if first else refs.pop(0)
    cos_ref, sin_ref = (refs.pop(0), refs.pop(0)) if last else (None, None)
    dq_ref = refs.pop(0)
    dkv_refs = [refs.pop(0) for _ in dists]
    dq_sc, dkv_sc = refs
    i = pl.program_id(0)
    place = i % per_pair
    half = place // (per_pair // 2)
    count = info_ref[0]
    q = q_ref[...]
    do = do_ref[...]
    rows = q.shape[0]

    @pl.when(place == 0)
    def _():
        dkv_sc[...] = jnp.zeros_like(dkv_sc)

    dq_sc[...] = jnp.zeros_like(dq_sc) if first else before_ref[0]
    prod = (do.astype(F32) * o_ref[...].astype(F32)).T
    deltas = [
        jnp.sum(prod[h * HD : (h + 1) * HD], axis=0, keepdims=True) for h in range(2)
    ]
    qs = placed_views(q, half)
    ds_ = placed_views(do, half)

    def part(at, s):
        kv = kv_refs[at]
        ks = half_views(kv[:, :LANES], half)
        vs = half_views(kv[:, LANES:], half)
        for h in range(2):
            scores = mm(ks[h], q, NT)
            chance = jnp.exp(scores - lse_ref[0, h : h + 1, :])
            if s == 0:
                key_at = lax.broadcasted_iota(jnp.int32, scores.shape, 0)
                row_at = lax.broadcasted_iota(jnp.int32, scores.shape, 1)
                chance = jnp.where(key_at <= row_at, chance, 0.0)
            d_chance = mm(vs[h], do, NT)
            d_scores = (chance * (d_chance - deltas[h])).astype(BF)
            dkv_sc[at, :, :LANES] += mm(d_scores, qs[h])
            dkv_sc[at, :, LANES:] += mm(chance.astype(BF), ds_[h])
            dq_sc[...] += mm(ks[h], d_scores, TN)

    for at, s in enumerate(dists):
        if s == 0:
            part(at, s)
        else:
            pl.when(s <= count)(functools.partial(part, at, s))

    if last:
        dq = dq_sc[...].T * score_scale
        dq_ref[...] = turn(dq, cos_ref[...], -sin_ref[...]).astype(BF)
    else:
        dq_ref[0] = dq_sc[...]

    @pl.when(place == per_pair - 1)
    def _():
        for at in range(len(dists)):
            dkv_refs[at][...] = dkv_sc[at].astype(BF)


def bwd_call(info, q, do, o, lse, kvs, dists, before, tables):
    rows, width = q.shape
    tiles = width // LANES
    wide = kvs[0].shape[1]
    per_pair = tiles // (wide // (2 * LANES))
    first, last = before is None, tables is not None
    col = pl.BlockSpec((rows, LANES), lambda i, _: (0, i))
    pair = pl.BlockSpec((rows, 2 * LANES), lambda i, _: (0, i // per_pair))
    turned = pl.BlockSpec((1, LANES, rows), lambda i, _: (i, 0, 0))
    fixed = pl.BlockSpec((rows, LANES), lambda i, _: (0, 0))
    m = len(dists)
    extra = [] if first else [before]
    extra += list(tables) if last else []
    return call(
        functools.partial(bwd_body, dists=dists, per_pair=per_pair, first=first, last=last),
        flops=10 * rows * rows * m * width,
        nbytes=10 * rows * width + 4 * m * rows * wide,
        trans=rows * rows * m * width // HD,
        grid_spec=pltpu.PrefetchScalarGridSpec(
            num_scalar_prefetch=1,
            grid=(tiles,),
            in_specs=[col, col, col, pl.BlockSpec((1, 8, rows), lambda i, _: (i, 0, 0))]
            + [pair] * m
            + ([] if first else [turned])
            + ([fixed, fixed] if last else []),
            out_specs=[col if last else turned] + [pair] * m,
            scratch_shapes=[
                pltpu.VMEM((LANES, rows), F32),
                pltpu.VMEM((m, rows, 2 * LANES), F32),
            ],
        ),
        out_shape=[
            jax.ShapeDtypeStruct((rows, width), BF)
            if last
            else jax.ShapeDtypeStruct((tiles, LANES, rows), F32)
        ]
        + [jax.ShapeDtypeStruct((rows, wide), BF)] * m,
        name="attend_back",
    )(info, q, do, o, lse, *[kvs[s] for s in dists], *extra)


def unturn_body(a_ref, b_ref, cos_ref, sin_ref, o_ref):
    t = a_ref[...].astype(F32) + b_ref[...].astype(F32)
    o_ref[:, :LANES] = turn(t[:, :LANES], cos_ref[...], -sin_ref[...]).astype(BF)
    o_ref[:, LANES:] = t[:, LANES:].astype(BF)


def unturn_call(a, b, cos_t, sin_t):
    rows, wide = a.shape
    blk = pl.BlockSpec((rows, 2 * LANES), lambda i: (0, i))
    fixed = pl.BlockSpec((rows, LANES), lambda i: (0, 0))
    return call(
        unturn_body,
        flops=8 * rows * wide,
        nbytes=6 * rows * wide,
        grid=(wide // (2 * LANES),),
        in_specs=[blk, blk, fixed, fixed],
        out_specs=blk,
        out_shape=jax.ShapeDtypeStruct((rows, wide), BF),
        name="unturn",
    )(a, b, cos_t, sin_t)


def out_body(o_ref, w_ref, x_ref, gain_ref, mid_ref, n2_ref, acc):
    j = pl.program_id(0)
    _, n, wr, cols = w_ref.shape
    acc[j] = mm(o_ref[...], w_ref[...].reshape(n * wr, cols))

    @pl.when(j == pl.num_programs(0) - 1)
    def _():
        parts = acc.shape[0]
        total = None
        for p in range(parts):
            at = slice(p * cols, (p + 1) * cols)
            mid = x_ref[:, at].astype(F32) + acc[p]
            mid_ref[:, at] = mid
            piece = jnp.sum(mid * mid, axis=1, keepdims=True)
            total = piece if total is None else total + piece
        inv = lax.rsqrt(total / (parts * cols) + norm_eps)
        for p in range(parts):
            at = slice(p * cols, (p + 1) * cols)
            n2_ref[:, at] = (mid_ref[:, at] * inv * gain_ref[:, at]).astype(BF)


def out_call(o, wo, x, gain):
    rows, width = x.shape
    dps, n, wr, cols = wo.shape
    full = pl.BlockSpec((rows, width), lambda j: (0, 0))
    return call(
        out_body,
        flops=2 * rows * width * n * wr,
        nbytes=2 * width * n * wr + 12 * rows * width,
        grid=(dps,),
        in_specs=[
            pl.BlockSpec((rows, n * wr), lambda j: (0, 0)),
            pl.BlockSpec((1, n, wr, cols), lambda j: (j, 0, 0, 0)),
            full,
            pl.BlockSpec((1, width), lambda j: (0, 0)),
        ],
        out_specs=[full, full],
        out_shape=[
            jax.ShapeDtypeStruct((rows, width), F32),
            jax.ShapeDtypeStruct((rows, width), BF),
        ],
        scratch_shapes=[pltpu.VMEM((dps, rows, cols), F32)],
        name="out_proj",
    )(o, wo, x, gain)


def ffn_body(n2_ref, g_ref, wg_ref, wu_ref, wd_ref, *refs, first):
    if not first:
        refs = refs[5:]
    n2_all, g_all, hid_all, dg_all, du_all, ffn_ref, dn_ref, ffn_acc, dn_acc = refs
    f = pl.program_id(0)
    n2 = n2_ref[...]
    g = g_ref[...]

    @pl.when(f == 0)
    def _():
        n2_all[...] = n2
        g_all[...] = g

    wg, wu, wd = wg_ref[...], wu_ref[...], wd_ref[...]
    gate = mm(n2, wg)
    up = mm(n2, wu)
    d_hid = mm(g, wd, NT)
    sig = jax.nn.sigmoid(gate)
    act = gate * sig
    hid = (act * up).astype(BF)
    d_gate = (d_hid * up * sig * (1.0 + gate * (1.0 - sig))).astype(BF)
    d_up = (d_hid * act).astype(BF)
    hid_all[...] = hid
    dg_all[...] = d_gate
    du_all[...] = d_up
    ffn = mm(hid, wd)
    dn = mm(d_gate, wg, NT) + mm(d_up, wu, NT)

    @pl.when(f == 0)
    def _():
        ffn_acc[...] = ffn
        dn_acc[...] = dn

    @pl.when(f > 0)
    def _():
        ffn_acc[...] += ffn
        dn_acc[...] += dn

    @pl.when(f == pl.num_programs(0) - 1)
    def _():
        ffn_ref[...] = ffn_acc[...].astype(BF)
        dn_ref[...] = dn_acc[...].astype(BF)


def ffn_call(n2, g, wg, wu, wd, s, n, big):
    rows, width = n2.shape
    ff = wg.shape[1]
    tf = min(512, ff)
    first = big is None
    full = pl.BlockSpec((rows, width), lambda f: (0, 0))
    wcol = pl.BlockSpec((width, tf), lambda f: (0, f))
    wide_all = pl.BlockSpec((rows, width), lambda f: (s, 0))
    tile_all = pl.BlockSpec((rows, tf), lambda f: (s, f))
    any_spec = pl.BlockSpec(memory_space=pl.ANY)
    out = call(
        functools.partial(ffn_body, first=first),
        flops=12 * rows * width * ff,
        nbytes=6 * width * ff + 12 * rows * width + 6 * rows * ff,
        grid=(ff // tf,),
        in_specs=[full, full, wcol, wcol, pl.BlockSpec((tf, width), lambda f: (f, 0))]
        + ([] if first else [any_spec] * 5),
        out_specs=[wide_all, wide_all, tile_all, tile_all, tile_all, full, full],
        out_shape=[jax.ShapeDtypeStruct((n * rows, width), BF)] * 2
        + [jax.ShapeDtypeStruct((n * rows, ff), BF)] * 3
        + [jax.ShapeDtypeStruct((rows, width), BF)] * 2,
        scratch_shapes=[pltpu.VMEM((rows, width), F32), pltpu.VMEM((rows, width), F32)],
        input_output_aliases={} if first else {5 + k: k for k in range(5)},
        name="ffn",
    )(n2, g, wg, wu, wd, *([] if first else big))
    return out[:5], out[5], out[6]


def do_body(da_ref, w_ref, do_ref):
    dps, _, wr, cols = w_ref.shape
    total = None
    for p in range(dps):
        piece = mm(da_ref[:, p * cols : (p + 1) * cols], w_ref[p, 0], NT)
        total = piece if total is None else total + piece
    do_ref[...] = total.astype(BF)


def do_call(da, wo):
    rows, width = da.shape
    dps, n, wr, cols = wo.shape
    return call(
        do_body,
        flops=2 * rows * width * n * wr,
        nbytes=2 * width * n * wr + 4 * rows * width,
        grid=(n,),
        in_specs=[
            pl.BlockSpec((rows, width), lambda j: (0, 0)),
            pl.BlockSpec((dps, 1, wr, cols), lambda j: (0, j, 0, 0)),
        ],
        out_specs=pl.BlockSpec((rows, wr), lambda j: (0, j)),
        out_shape=jax.ShapeDtypeStruct((rows, n * wr), BF),
        name="d_o",
    )(da, wo)


def dn1_body(dq_ref, dkv_ref, w_ref, out_ref, *, qc):
    _, n, wr, cols = w_ref.shape
    kc2 = cols - qc
    total = None
    for j in range(n):
        w = w_ref[0, j]
        piece = mm(dq_ref[:, j * qc : (j + 1) * qc], w[:, :qc], NT) + mm(
            dkv_ref[:, j * kc2 : (j + 1) * kc2], w[:, qc:], NT
        )
        total = piece if total is None else total + piece
    out_ref[...] = total


def dn1_call(dq, dkv, wqkv, qc):
    rows = dq.shape[0]
    dps, n, wr, cols = wqkv.shape
    return call(
        functools.partial(dn1_body, qc=qc),
        flops=2 * rows * dps * wr * n * cols,
        nbytes=2 * dps * wr * n * cols + 4 * rows * dps * wr,
        grid=(dps,),
        in_specs=[
            pl.BlockSpec(dq.shape, lambda p: (0, 0)),
            pl.BlockSpec(dkv.shape, lambda p: (0, 0)),
            pl.BlockSpec((1, n, wr, cols), lambda p: (p, 0, 0, 0)),
        ],
        out_specs=pl.BlockSpec((rows, wr), lambda p: (0, p)),
        out_shape=jax.ShapeDtypeStruct((rows, dps * wr), F32),
        name="d_n1",
    )(dq, dkv, wqkv)


def dw_body(blk_ref, l0_ref, l1_ref, r_ref, *refs, add):
    add_ref = refs[0] if add else None
    out_ref, left = refs[-2:]
    wr = l0_ref.shape[1]

    @pl.when(pl.program_id(1) == 0)
    def _():
        left[:wr] = l0_ref[...].T
        left[wr:] = l1_ref[...].T

    y = mm(left[...], r_ref[...])
    for k in range(2):
        part = y[k * wr : (k + 1) * wr]
        if add:
            part = part + add_ref[k].astype(F32)
        out_ref[k] = part.astype(BF)


def dw_call(blocks, lhs, rhs, wr, extra):
    half = blocks.shape[0]
    toks, cols = lhs.shape[0], rhs.shape[1]
    tn = min(cols, 512 if toks > 1024 else 1024)
    out = pl.BlockSpec((2, wr, tn), lambda t, c, _: (t, 0, c))
    return call(
        functools.partial(dw_body, add=extra is not None),
        flops=2 * toks * cols * half * wr,
        nbytes=2 * (toks * cols + half * wr * (toks + 2 * cols)),
        grid_spec=pltpu.PrefetchScalarGridSpec(
            num_scalar_prefetch=1,
            grid=(half // 2, cols // tn),
            in_specs=[
                pl.BlockSpec((toks, wr), lambda t, c, blk: (0, blk[2 * t])),
                pl.BlockSpec((toks, wr), lambda t, c, blk: (0, blk[2 * t + 1])),
                pl.BlockSpec((toks, tn), lambda t, c, _: (0, c)),
            ]
            + ([] if extra is None else [out]),
            out_specs=out,
            scratch_shapes=[pltpu.VMEM((2 * wr, toks), BF)],
        ),
        out_shape=jax.ShapeDtypeStruct((half, wr, cols), BF),
        name="dw",
    )(blocks, lhs, lhs, rhs, *([] if extra is None else [extra]))


def norm_back(values, inv_root, gain_vec, d_norm):
    scaled = d_norm * gain_vec
    inner_sum = jnp.mean(scaled * values, axis=-1, keepdims=True)
    d_values = inv_root * scaled - values * (inv_root * inv_root * inv_root) * inner_sum
    return (d_values, jnp.sum(d_norm * values * inv_root, axis=0))


def plus(a, b):
    return (a.astype(F32) + b.astype(F32)).astype(BF)


def advance(main, tasks):
    held = [task[1] for task in tasks]
    main, held = lax.optimization_barrier((main, held))
    for task, values in zip(tasks, held):
        if task[1]:
            try:
                task[1] = task[0].send(values)
            except StopIteration as end:
                task[1], task[2] = [], end.value
    return main


def task_of(steps):
    return [steps, next(steps), None]


def finish(task):
    while task[1]:
        try:
            task[1] = task[0].send(task[1])
        except StopIteration as end:
            task[1], task[2] = [], end.value
    return task[2]


def spread_sum(x, name, size):
    step = 1
    while step < size:
        x = x + lax.ppermute(x, name, [(i, i ^ step) for i in range(size)])
        step *= 2
    return x


def per_device(
    tokens,
    segment_ids,
    grad_out,
    attn_gain,
    w_query,
    w_key,
    w_value,
    w_output,
    ffn_gain,
    w_gate,
    w_up,
    w_down,
    *,
    dps,
    n,
):
    rows, width = tokens.shape
    qc, kc = w_query.shape[1], w_key.shape[1]
    zi = lax.axis_index("mp")
    di = lax.axis_index("dp")
    ring = [(i, (i + 1) % n) for i in range(n)]
    up_chain = [(i, i + 1) for i in range(n - 1)]
    down_chain = [(i + 1, i) for i in range(n - 1)]
    x = tokens.astype(F32)
    gain_one = attn_gain.astype(F32)
    gain_two = ffn_gain.astype(F32)

    wr = width // dps
    piece = jnp.concatenate(
        [lax.dynamic_slice_in_dim(w, di * wr, wr, 0) for w in (w_query, w_key, w_value)], axis=1
    )
    wqkv = lax.all_gather(piece, ("dp", "mp"), axis=0).reshape(dps, n, wr, qc + 2 * kc)
    oc = width // dps
    wo_piece = lax.dynamic_slice_in_dim(w_output, di * oc, oc, 1)
    wo = lax.all_gather(wo_piece, ("dp", "mp"), axis=0).reshape(dps, n, w_output.shape[0], oc)

    row_index = zi * rows + jnp.arange(rows, dtype=jnp.int32)
    own_seg = lax.dynamic_slice_in_dim(segment_ids, zi * rows, rows, 0)
    first_row = jnp.sum((segment_ids[None, :] < own_seg[:, None]).astype(jnp.int32), axis=1)
    cos_t, sin_t = rope_table((row_index - first_row).astype(F32))
    count = zi - first_row[0] // rows
    info = jnp.reshape(count, (1,)).astype(jnp.int32)

    inv_one = lax.rsqrt(jnp.mean(x * x, axis=-1, keepdims=True) + norm_eps)
    n1 = (x * inv_one * gain_one).astype(BF)

    gs = [grad_out]
    for s in range(1, n - 1):
        gs.append(lax.ppermute(gs[-1], "mp", ring))
    n1, *gs = lax.optimization_barrier((n1, *gs))
    q, kv = qkv_call(n1, wqkv, cos_t, sin_t, qc, kc)
    if kc < LANES:
        fold = LANES // kc
        kv = (
            kv.reshape(rows, n // fold, fold, 2, kc)
            .transpose(0, 1, 3, 2, 4)
            .reshape(rows, n * 2 * kc)
        )
    kvs = [kv]
    for s in range(1, n):
        kvs.append(lax.ppermute(kvs[-1], "mp", up_chain))
    late, kvs[-1] = lax.optimization_barrier((gs[-1], kvs[-1]))
    gs.append(lax.ppermute(late, "mp", ring))

    o, lse = fwd_call(info, q, kvs)
    mid, n2 = out_call(o, wo, tokens, gain_two.reshape(1, width))

    n2s = [n2]
    for s in range(1, n):
        n2s.append(lax.ppermute(n2s[-1], "mp", ring))
    big, t, own_dn = None, None, None
    ffn_parts = []
    for s in range(n):
        n2c = n2s[s]
        if s >= 3:
            n2c, t = lax.optimization_barrier((n2c, t))
        big, part, dn = ffn_call(n2c, gs[s], w_gate, w_up, w_down, s, n, big)
        ffn_parts.append(part)
        if s == 0:
            own_dn = dn
        elif s == 1:
            t = dn
        elif s < n - 1:
            t = plus(lax.ppermute(t, "mp", ring), dn)
    n2_all, g_all, hid_all, dg_all, du_all = big

    core = di % 2
    pairs = jnp.arange(dps // 2, dtype=jnp.int32) * 2
    fixed_ids = [pairs + (core ^ c) for c in range(2)]
    swap = [(i, i ^ 1) for i in range(dps)]
    jobs = ((n2_all, dg_all), (n2_all, du_all), (g_all, hid_all))
    got = lax.ppermute(t, "mp", ring)
    away = [dw_call(fixed_ids[1], a, b, wr, None) for a, b in jobs]
    got, away = lax.optimization_barrier((got, away))
    got = lax.ppermute(plus(got, dn), "mp", ring)
    away = [lax.ppermute(a, "dp", swap) for a in away]
    kept = [dw_call(fixed_ids[0], a, b, wr, e) for (a, b), e in zip(jobs, away)]
    got, kept = lax.optimization_barrier((got, kept))
    d_n2 = got.astype(F32) + own_dn.astype(F32)
    d_n2, ffn_parts = lax.optimization_barrier((d_n2, ffn_parts))

    def ffn_ring():
        t = ffn_parts[1]
        for s in range(2, n):
            t = plus(lax.ppermute(t, "mp", ring), ffn_parts[s])
            (t,) = yield [t]
        t = lax.ppermute(t, "mp", ring)
        return (mid + t.astype(F32) + ffn_parts[0].astype(F32)).astype(BF)

    inv_two = lax.rsqrt(jnp.mean(mid * mid, axis=-1, keepdims=True) + norm_eps)
    d_from_two, gain_two_part = norm_back(mid, inv_two, gain_two, d_n2)
    d_mid = grad_out.astype(F32) + d_from_two
    da = d_mid.astype(BF)
    do = do_call(da, wo)

    moving_ids = [di ^ (pairs + c) for c in range(2)]

    def cube(lhs, rhs):
        away = lax.ppermute(dw_call(moving_ids[1], lhs, rhs, wr, None), "dp", swap)
        near = dw_call(moving_ids[0], lhs, rhs, wr, away)
        (near,) = yield [near]
        bits = (dps // 2).bit_length() - 1
        wide = near.shape[2] // 2
        ts = [
            near[:, :, k * wide : (k + 1) * wide].reshape((2,) * bits + (wr, wide))
            for k in range(2)
        ]
        left = [list(range(bits)), list(range(bits))]
        for step in range(bits):
            for k in range(2):
                bit = left[k][-1 if k else 0]
                axis = left[k][::-1].index(bit)
                left[k].remove(bit)
                perm = [(i, i ^ (2 << bit)) for i in range(dps)]
                away = lax.ppermute(
                    lax.index_in_dim(ts[k], 1, axis, keepdims=False), "dp", perm
                )
                ts[k] = plus(lax.index_in_dim(ts[k], 0, axis, keepdims=False), away)
            ts = yield ts
        return jnp.concatenate(ts, axis=1).reshape(wr, n, -1)

    two_core = [[i for i in range(dps) if i % 2 == c] for c in range(2)]

    def over_dp(g):
        return lax.psum_scatter(
            g, "dp", scatter_dimension=0, axis_index_groups=two_core, tiled=False
        ).astype(F32)

    gate_sum, up_sum, down_sum = [over_dp(g) for g in kept]
    wo_task = task_of(cube(da, o))
    ffn_task = task_of(ffn_ring())
    before = None
    travel = None
    for at, s in enumerate(reversed(range(n))):
        tables = (cos_t, sin_t) if s == 0 else None
        before, dkv = bwd_call(info, q, do, o, lse, kvs, (s,), before, tables)
        if travel is not None and s > 0:
            dkv = plus(lax.ppermute(travel, "mp", down_chain), dkv)
        tasks = [wo_task] + ([ffn_task] if at % 2 else [])
        if s > 0:
            before, travel = advance((before, dkv), tasks)
        else:
            before, dkv = advance((before, dkv), tasks)
            dkv_own = unturn_call(lax.ppermute(travel, "mp", down_chain), dkv, cos_t, sin_t)
    dq = before
    wo_cube = finish(wo_task)
    if kc < LANES:
        dkv_own = (
            dkv_own.reshape(rows, n // fold, 2, fold, kc)
            .transpose(0, 1, 3, 2, 4)
            .reshape(rows, n * 2 * kc)
        )
    cubes = [finish(task_of(cube(n1, dq))), finish(task_of(cube(n1, dkv_own))), wo_cube]
    w_cube = jnp.concatenate(cubes, axis=2)
    d_n1 = dn1_call(dq, dkv_own, wqkv, qc)
    layer_out = finish(ffn_task)
    d_from_one, gain_one_part = norm_back(x, inv_one, gain_one, d_n1)
    grad_tokens = (d_mid + d_from_one).astype(BF)

    gains = jnp.stack([gain_one_part, gain_two_part])
    gains = spread_sum(spread_sum(gains, "mp", n), "dp", dps)

    def over_mp(g):
        return lax.psum_scatter(g, "mp", scatter_dimension=1, tiled=False).astype(F32)

    w_sum = over_mp(w_cube)
    cols = qc + 2 * kc
    return (
        layer_out,
        grad_tokens,
        gains[0],
        w_sum[:, :qc],
        w_sum[:, qc : qc + kc],
        w_sum[:, qc + kc : cols],
        w_sum[:, cols:].T,
        gains[1],
        gate_sum,
        up_sum,
        down_sum.T,
    )


def solution(mesh):
    rows = P(("dp", "mp"), None)
    col = P(None, "mp")
    row = P("mp", None)
    placed = (rows, P("dp"), rows, P(), col, col, col, row, P(), col, col, row)
    body = functools.partial(per_device, dps=mesh.shape["dp"], n=mesh.shape["mp"])
    return jax.shard_map(
        body,
        mesh=mesh,
        in_specs=placed,
        out_specs=(
            rows,
            rows,
            P(),
            P("dp", "mp"),
            P("dp", "mp"),
            P("dp", "mp"),
            P("mp", "dp"),
            P(),
            P("dp", "mp"),
            P("dp", "mp"),
            P("mp", "dp"),
        ),
        check_vma=False,
    )
```
